32 devices in a mesh: lag: 4 (over y, core), row: 8 (over z, x).
Axes of the slice: x: 2, y: 2, z: 4, core: 2. Of those that a mesh axis runs over, the one named last changes fastest.
Arguments:
- lag_ops: float32 [8, 3072, 3072], P('lag', 'row'), may hold values from -0.109375 to 0.109375
- inverse: float32 [3072, 3072], P('row'), may hold values from -0.109375 to 0.109375
- history: float32 [8, 3072, 128], P('lag', 'row'), may hold values from -6 to 6
- loads: float32 [3, 3072, 128], P(None, 'row'), may hold values from -6 to 6
Outputs:
- current: float32 [3072, 128], P('row')
- future: float32 [8, 3072, 128], P('lag', 'row')
The draws below stay inside these ranges and needn't reach their ends.
All inputs are finite; a program needn't handle non-finite values.
Results may differ from the reference program's by a relative error of at most 0.00011.
Values sent between devices are 32-bit elements; how exact they have to be, the bound alone decides.
No kernel may reach another device: no remote copies, remote signals or barrier semaphores. Data moves between devices by JAX's collectives and lax.ppermute only.
A program may use at most 64 MiB of HBM per device.

```python
import jax
import jax.numpy as jnp
from jax import lax

U = 3072
LOADS = 128
STEPS = 3
LAGS = 8


def block_levels(stream_key, dims, cuts, least, high):
    def one(dim, shards_of):
        draws = jax.random.uniform(jax.random.fold_in(jax.random.fold_in(stream_key, 6), dim), (shards_of,), jnp.float32, least / len(cuts), high / len(cuts))
        return jnp.repeat(jnp.exp(draws), dims[dim] // shards_of).reshape((-1,) + (1,) * (len(dims) - dim - 1))

    level = one(*cuts[0])
    for cut in cuts[1:]:
        level = level * one(*cut)
    return level


def normal_values(stream_key, dims, scale, reach, cuts=(), held_as=jnp.bfloat16):
    values = jax.random.normal(stream_key, dims, jnp.float32) * scale
    if len(cuts) > 0:
        values = block_levels(stream_key, dims, cuts, -0.22, 0.18) * values
    return jnp.clip(values, min=-reach, max=reach).astype(held_as)


def setup_inputs(seed: int = 0) -> dict:
    arg_keys = jax.random.split(jax.random.key(seed), 5)
    return {
        "lag_ops": normal_values(arg_keys[0], (LAGS, U, U), U ** -0.5, 0.109375, ((0, 4), (1, 8)), jnp.float32),
        "inverse": normal_values(arg_keys[1], (U, U), U ** -0.5, 0.109375, ((0, 8),), jnp.float32),
        "history": normal_values(arg_keys[2], (LAGS, U, LOADS), 1.0, 6.0, ((0, 4), (1, 8)), jnp.float32),
        "loads": normal_values(arg_keys[3], (STEPS, U, LOADS), 1.0, 6.0, ((1, 8),), jnp.float32),
    }


def reference(lag_ops, inverse, history, loads):
    acc = history
    current = jnp.zeros((U, LOADS), jnp.float32)
    for step in range(STEPS):
        rhs = loads[step] - acc[0]
        current = jnp.dot(inverse, rhs, precision=lax.Precision.HIGHEST, preferred_element_type=jnp.float32)
        product = jnp.einsum("kuv,vb->kub", lag_ops, current, precision=lax.Precision.HIGHEST)
        shifted = jnp.concatenate([acc[1:], jnp.zeros((1, U, LOADS), jnp.float32)], axis=0)
        acc = shifted + product
    return current, acc
```

```python
import jax
import jax.numpy as jnp
from jax import lax
from jax.sharding import PartitionSpec as P

STEPS = 3
AXES = ("lag", "row")


def broadcast(array, axis, root):
    mine = lax.axis_index(axis) == root
    return lax.psum(jnp.where(mine, array, jnp.zeros_like(array)), axis)


def from_behind(array, axis, by):
    length = lax.axis_size(axis)
    pairs = [(i, i + by) for i in range(length) if 0 <= i + by < length]
    return lax.ppermute(array, axis, pairs)


def plain_body(lag_ops, inverse, history, loads):
    acc = history
    local_lags = lag_ops.shape[0]
    local_rows = lag_ops.shape[1]
    total_cols = lag_ops.shape[2]
    loads_width = history.shape[2]
    flat_ops = lag_ops.reshape(local_lags * local_rows, total_cols)
    current = jnp.zeros((local_rows, loads_width), jnp.float32)
    for step in range(STEPS):
        rhs = broadcast(loads[step] - acc[0], "lag", 0)
        width = loads_width // lax.axis_size("lag")
        offset = lax.axis_index("lag") * width
        rhs_part = lax.dynamic_slice_in_dim(rhs, offset, width, 1)
        partial_value = jnp.dot(
            inverse,
            lax.all_gather(rhs_part, "row", axis=0, tiled=True),
            precision=lax.Precision.HIGHEST,
            preferred_element_type=jnp.float32,
        )
        current = lax.all_gather(partial_value, "lag", axis=1, tiled=True)
        product = jnp.dot(
            flat_ops,
            lax.all_gather(current, "row", axis=0, tiled=True),
            precision=lax.Precision.HIGHEST,
            preferred_element_type=jnp.float32,
        )
        product = product.reshape(local_lags, local_rows, loads_width)
        incoming = from_behind(acc[0], "lag", -1)
        shifted = jnp.concatenate([acc[1:], incoming[None]], axis=0)
        acc = shifted + product
    return (current, acc)


def swap(array, lag_bits, row_bits):
    lags, rows = lax.axis_size("lag"), lax.axis_size("row")
    pairs = [
        (g * rows + r, (g ^ lag_bits) * rows + (r ^ row_bits))
        for g in range(lags)
        for r in range(rows)
    ]
    return lax.ppermute(array, AXES, pairs)


def split(array):
    high = lax.reduce_precision(array, 8, 7)
    return high.astype(jnp.bfloat16), (array - high).astype(jnp.bfloat16)


def contract(a, b):
    return lax.dot_general(
        a, b, (((1,), (1,)), ((), ())), preferred_element_type=jnp.float32
    )


def product(vector, matrix):
    vh, vl = vector
    mh, ml = matrix
    n = vh.shape[0]
    both = contract(jnp.concatenate([vh, vl], 0), mh)
    return both[:n] + both[n:] + contract(vh, ml)


def quad_body(lag_ops, inverse, history, loads):
    rows_n = lax.axis_size("row")
    height = lag_ops.shape[1]
    half = height // 2
    width = loads.shape[2] // 4
    g = lax.axis_index("lag")
    r = lax.axis_index("row")
    plane, core = g // 2, g % 2
    near = [k for k in range(0, rows_n, 2)]
    order = near + [k + 1 for k in near]
    cut = len(near) * height

    def blocks(matrix):
        return jnp.concatenate(
            [lax.dynamic_slice_in_dim(matrix, (r ^ k) * height, height, 1) for k in order], 1
        )

    def halves(pair):
        return [tuple(p[:, :cut] for p in pair), tuple(p[:, cut:] for p in pair)]

    def gather(v):
        a = jnp.concatenate([v] + [swap(v, 0, k) for k in near[1:]], 1)
        return a, swap(a, 0, 1)

    def by_core(mine, other, axis):
        return jnp.where(
            core == 0,
            jnp.concatenate([mine, other], axis),
            jnp.concatenate([other, mine], axis),
        )

    hist = jnp.swapaxes(history, 1, 2)
    ops0, ops1 = lag_ops[0], lag_ops[1]

    def scatter_plane(a):
        got = swap(a[2 * width :], 2, 0)
        return jnp.where(plane == 0, a[: 2 * width], got)

    def scatter_core(a):
        keep = lax.dynamic_slice_in_dim(a, core * width, width, 0)
        give = lax.dynamic_slice_in_dim(a, (1 - core) * width, width, 0)
        return keep, swap(give, 1, 0)

    keep, got = scatter_core(scatter_plane(hist[0]))
    past0 = jnp.where(core == 0, keep, got)
    past2 = jnp.where(core == 0, got, keep)
    keep, got = scatter_core(scatter_plane(hist[1]))
    past1 = jnp.where(core == 0, keep, got)

    cols = jnp.swapaxes(lax.dynamic_slice_in_dim(loads, g * width, width, 2), 1, 2)

    inv = halves(split(blocks(inverse)))

    def solve(rhs):
        a, b = gather(rhs)
        return product(split(a), inv[0]) + product(split(b), inv[1])

    def core_half(ops):
        got = swap(ops[half:], 1, 0)
        return jnp.where(core == 0, ops[:half], got)

    mine0 = core_half(ops0)
    mine0 = jnp.where(plane == 0, mine0, swap(mine0, 2, 0))
    lead0 = halves(split(blocks(mine0)))
    lead1 = split(blocks(core_half(ops1)))
    whole = split(blocks(lag_ops.reshape(2 * height, -1)))

    def pair_up(cur):
        a, b = gather(cur)
        a = jnp.concatenate([a, swap(a, 1, 0)], 0)
        b = jnp.concatenate([b, swap(b, 1, 0)], 0)
        return a, b

    def full(a, b):
        v = jnp.concatenate([a, b], 1)
        far = swap(v[:width], 2, 0)
        far = by_core(far, swap(far, 1, 0), 0)
        near_ = by_core(v[:width], v[width:], 0)
        return jnp.where(
            plane == 0,
            jnp.concatenate([near_, far], 0),
            jnp.concatenate([far, near_], 0),
        )

    def lead(a, b):
        return product(split(a), lead0[0]) + product(split(b), lead0[1])

    def rejoin(part):
        return by_core(part[:width], swap(part[width:], 1, 0), 1)

    def behind(array):
        near_, far = swap(array, 1, 0), swap(array, 3, 0)
        return jnp.where(core == 0, near_, jnp.where(plane == 0, far, 0.0))

    def field(cur):
        ch, cl = split(cur)
        n = ch.shape[0]
        both = contract(whole[0], jnp.concatenate([ch, cl], 0))
        out = both[:, :n] + both[:, n:] + contract(whole[1], ch)
        return out.reshape(2, height, n)

    cur0 = solve(cols[0] - past0)
    a0, b0 = pair_up(cur0)
    rhs1 = cols[1] - past1 - rejoin(lead(a0, b0))
    full0 = full(a0, b0)
    second = product(split(full0), lead1)
    sent = jnp.where(plane == 0, second[2 * width :], second[: 2 * width])
    got = swap(sent, 2, 0)
    second = jnp.where(plane == 0, second[: 2 * width], got)
    second = jnp.where(
        core == 0, second, jnp.concatenate([second[width:], second[:width]], 0)
    )
    cur1 = solve(rhs1)
    a1, b1 = pair_up(cur1)
    rhs2 = cols[2] - past2 - rejoin(lead(a1, b1) + second)
    full1 = full(a1, b1)
    f0 = field(full0)
    acc = [history[1] + f0[0], behind(history[0]) + f0[1]]
    f1 = field(full1)
    acc = [acc[1] + f1[0], behind(acc[0]) + f1[1]]
    ahead = behind(acc[0])
    cur2 = solve(rhs2)
    full2 = full(*pair_up(cur2))
    f2 = field(full2)
    future = jnp.stack([acc[1] + f2[0], ahead + f2[1]], 0)
    return full2[:, :height].T, future


def solution(mesh):
    placed = (P("lag", "row", None), P("row", None), P("lag", "row", None), P(None, "row", None))

    def body(lag_ops, inverse, history, loads):
        lags, rows = lax.axis_size("lag"), lax.axis_size("row")
        fits = (
            lags == 4
            and lag_ops.shape[0] == STEPS - 1
            and rows & (rows - 1) == 0
            and lag_ops.shape[1] * rows == lag_ops.shape[2]
            and loads.shape[0] == STEPS
        )
        return (quad_body if fits else plain_body)(lag_ops, inverse, history, loads)

    return jax.shard_map(
        body,
        mesh=mesh,
        in_specs=placed,
        out_specs=(P("row", None), P("lag", "row", None)),
        check_vma=False,
    )
```

```python
import functools

import jax
import jax.numpy as jnp
from jax import lax
from jax.experimental import pallas as pl
from jax.experimental.pallas import tpu as pltpu
from jax.sharding import PartitionSpec as P

STEPS = 3
AXES = ("lag", "row")


def broadcast(array, axis, root):
    mine = lax.axis_index(axis) == root
    return lax.psum(jnp.where(mine, array, jnp.zeros_like(array)), axis)


def from_behind(array, axis, by):
    length = lax.axis_size(axis)
    pairs = [(i, i + by) for i in range(length) if 0 <= i + by < length]
    return lax.ppermute(array, axis, pairs)


def plain_body(lag_ops, inverse, history, loads):
    acc = history
    local_lags = lag_ops.shape[0]
    local_rows = lag_ops.shape[1]
    total_cols = lag_ops.shape[2]
    loads_width = history.shape[2]
    flat_ops = lag_ops.reshape(local_lags * local_rows, total_cols)
    current = jnp.zeros((local_rows, loads_width), jnp.float32)
    for step in range(STEPS):
        rhs = broadcast(loads[step] - acc[0], "lag", 0)
        width = loads_width // lax.axis_size("lag")
        offset = lax.axis_index("lag") * width
        rhs_part = lax.dynamic_slice_in_dim(rhs, offset, width, 1)
        partial_value = jnp.dot(
            inverse,
            lax.all_gather(rhs_part, "row", axis=0, tiled=True),
            precision=lax.Precision.HIGHEST,
            preferred_element_type=jnp.float32,
        )
        current = lax.all_gather(partial_value, "lag", axis=1, tiled=True)
        product = jnp.dot(
            flat_ops,
            lax.all_gather(current, "row", axis=0, tiled=True),
            precision=lax.Precision.HIGHEST,
            preferred_element_type=jnp.float32,
        )
        product = product.reshape(local_lags, local_rows, loads_width)
        incoming = from_behind(acc[0], "lag", -1)
        shifted = jnp.concatenate([acc[1:], incoming[None]], axis=0)
        acc = shifted + product
    return (current, acc)


def swap(array, lag_bits, row_bits):
    lags, rows = lax.axis_size("lag"), lax.axis_size("row")
    pairs = [
        (g * rows + r, (g ^ lag_bits) * rows + (r ^ row_bits))
        for g in range(lags)
        for r in range(rows)
    ]
    return lax.ppermute(array, AXES, pairs)


def split(array):
    high = lax.reduce_precision(array, 8, 7)
    return high.astype(jnp.bfloat16), (array - high).astype(jnp.bfloat16)


def split_here(array):
    high = array.astype(jnp.bfloat16)
    return high, (array - high.astype(jnp.float32)).astype(jnp.bfloat16)


def contract(a, b):
    return lax.dot_general(
        a, b, (((1,), (1,)), ((), ())), preferred_element_type=jnp.float32
    )


def product(vector, matrix):
    vh, vl = vector
    mh, ml = matrix
    n = vh.shape[0]
    both = contract(jnp.concatenate([vh, vl], 0), mh)
    return both[:n] + both[n:] + contract(vh, ml)


def turn_kernel(history_ref, loads_ref, past_ref, given_ref, rhs_ref):
    for i in range(past_ref.shape[0]):
        past_ref[i] = history_ref[i].T
    for i in range(given_ref.shape[0]):
        given_ref[i] = loads_ref[i].T
    rhs_ref[...] = given_ref[0] - past_ref[0]


def turn(history, loads):
    shapes = [
        jax.ShapeDtypeStruct((a.shape[0], a.shape[2], a.shape[1]), a.dtype)
        for a in (history, loads)
    ]
    return pl.pallas_call(
        turn_kernel,
        out_shape=(*shapes, jax.ShapeDtypeStruct(shapes[0].shape[1:], history.dtype)),
        compiler_params=pltpu.CompilerParams(vmem_limit_bytes=16 << 20),
        name="turn",
    )(history, loads)


def split_kernel(order_ref, m_ref, high_ref, low_ref):
    high_ref[...], low_ref[...] = split_here(m_ref[...])


def split_blocks(matrix, order, size):
    rows, cols = matrix.shape
    out = jax.ShapeDtypeStruct((rows, cols), jnp.bfloat16)
    spec = pl.BlockSpec((rows, size), lambda i, o: (0, i))
    return pl.pallas_call(
        split_kernel,
        out_shape=(out, out),
        grid_spec=pltpu.PrefetchScalarGridSpec(
            num_scalar_prefetch=1,
            grid=(cols // size,),
            in_specs=[pl.BlockSpec((rows, size), lambda i, o: (0, o[i]))],
            out_specs=(spec, spec),
        ),
        compiler_params=pltpu.CompilerParams(vmem_limit_bytes=16 << 20),
        cost_estimate=pl.CostEstimate(
            flops=0, bytes_accessed=8 * rows * cols, transcendentals=0
        ),
        name="split_blocks",
    )(order, matrix)


def field_kernel(flip, given, order_ref, m_ref, v_ref, base_ref, *refs):
    total_ref, last = refs[-1], pl.num_programs(0) - 1
    n = v_ref.shape[0]
    mh, ml = split_here(m_ref[0])
    vh, vl = split_here(v_ref[...])
    both = contract(jnp.concatenate([vh, vl], 0), mh)
    part = both[:n] + both[n:] + contract(vh, ml)

    @pl.when(pl.program_id(0) == 0)
    def _():
        total_ref[...] = base_ref[...] + part

    @pl.when(pl.program_id(0) > 0)
    def _():
        total_ref[...] += part

    @pl.when(pl.program_id(0) == last)
    def _():
        if given:
            given_ref, out_ref, rhs_ref, _ = refs
            out_ref[...] = total_ref[...]
            rhs_ref[...] = given_ref[0] - total_ref[...]
        else:
            out_ref = refs[0]
            out_ref[...] = total_ref[...].T if flip else total_ref[...]


def field(ops, lag, current, order, base, loads=None, step=0, flip=False):
    _, rows, cols = ops.shape
    n = current.shape[0]
    size = rows
    whole = pl.BlockSpec((n, rows), lambda i, o: (0, 0))
    shape = jax.ShapeDtypeStruct((n, rows), jnp.float32)
    inputs, in_specs = [order, ops, current, base], [
        pl.BlockSpec((1, rows, size), lambda i, o: (lag, 0, o[i])),
        pl.BlockSpec((n, size), lambda i, o: (0, i)),
        whole,
    ]
    out_shape, out_specs = shape, whole
    if flip:
        out_shape = jax.ShapeDtypeStruct((rows, n), jnp.float32)
        out_specs = pl.BlockSpec((rows, n), lambda i, o: (0, 0))
    if loads is not None:
        inputs.append(loads)
        in_specs.append(pl.BlockSpec((1, n, rows), lambda i, o: (step, 0, 0)))
        out_shape, out_specs = (shape, shape), (whole, whole)
    return pl.pallas_call(
        functools.partial(field_kernel, flip, loads is not None),
        out_shape=out_shape,
        grid_spec=pltpu.PrefetchScalarGridSpec(
            num_scalar_prefetch=1,
            grid=(cols // size,),
            in_specs=in_specs,
            out_specs=out_specs,
            scratch_shapes=[pltpu.VMEM((n, rows), jnp.float32)],
        ),
        compiler_params=pltpu.CompilerParams(vmem_limit_bytes=16 << 20),
        cost_estimate=pl.CostEstimate(
            flops=6 * rows * cols * n, bytes_accessed=4 * rows * cols, transcendentals=0
        ),
        name="field",
    )(*inputs)


def quad_body(lag_ops, inverse, history, loads):
    rows_n = lax.axis_size("row")
    height = lag_ops.shape[1]
    width = loads.shape[2] // 4
    g = lax.axis_index("lag")
    r = lax.axis_index("row")
    plane, core = g // 2, g % 2
    near = [k for k in range(0, rows_n, 2)]
    steps = near + [k + 1 for k in near]
    cut = len(near) * height
    order = r ^ jnp.array(steps, jnp.int32)
    lag_ops = pltpu.with_memory_space_constraint(lag_ops, pltpu.HBM)

    def line(v):
        return jnp.concatenate([v] + [swap(v, 0, k) for k in near[1:]], 1)

    def scatter(rhs):
        got = swap(rhs[2 * width :], 2, 0)
        pair = jnp.where(plane == 0, rhs[: 2 * width], got)
        got = swap(pair[width:], 1, 0)
        return jnp.where(core == 0, pair[:width], got)

    def full(a):
        b = swap(a, 0, 1)
        ya = swap(a, 2, 0)
        yb = swap(b, 2, 0)
        a, b = jnp.concatenate([a, ya], 0), jnp.concatenate([b, yb], 0)
        v = jnp.concatenate([a, b], 1)
        w = jnp.concatenate([swap(a, 1, 0), swap(b, 1, 0)], 1)
        chunks = [v[:width], w[:width], v[width:], w[width:]]
        even = [jnp.where(core == 0, chunks[j], chunks[j ^ 1]) for j in range(4)]
        return jnp.concatenate(
            [jnp.where(plane == 0, even[j], even[j ^ 2]) for j in range(4)], 0
        )

    def behind(array):
        near_, far = swap(array, 1, 0), swap(array, 3, 0)
        return jnp.where(core == 0, near_, jnp.where(plane == 0, far, 0.0))

    past, given, rhs = turn(history, loads)
    acc0, acc1 = past[0], past[1]
    inv = None
    for step in range(STEPS):
        rhs = scatter(rhs)
        if inv is None:
            rhs, inverse = lax.optimization_barrier((rhs, inverse))
            high, low = split_blocks(inverse, order, height)
            inv = [(high[:, :cut], low[:, :cut]), (high[:, cut:], low[:, cut:])]
        else:
            rhs, current = lax.optimization_barrier((rhs, current))
        a = line(rhs)
        a, acc0 = lax.optimization_barrier((a, acc0))
        ahead = behind(acc0)
        if step > 0:
            acc1 = field(lag_ops, 1, current, order, below)
        b = swap(a, 0, 1)
        solved = product(split(a), inv[0]) + product(split(b), inv[1])
        current = full(line(solved))
        below = ahead
        if step < STEPS - 1:
            acc0, rhs = field(lag_ops, 0, current, order, acc1, given, step + 1)
    future = [
        field(lag_ops, 0, current, order, acc1, flip=True),
        field(lag_ops, 1, current, order, below, flip=True),
    ]
    return current[:, :height].T, jnp.stack(future, 0)


def solution(mesh):
    placed = (P("lag", "row", None), P("row", None), P("lag", "row", None), P(None, "row", None))

    def body(lag_ops, inverse, history, loads):
        lags, rows = lax.axis_size("lag"), lax.axis_size("row")
        fits = (
            lags == 4
            and lag_ops.shape[0] == STEPS - 1
            and rows & (rows - 1) == 0
            and lag_ops.shape[1] * rows == lag_ops.shape[2]
            and loads.shape[0] == STEPS
        )
        return (quad_body if fits else plain_body)(lag_ops, inverse, history, loads)

    return jax.shard_map(
        body,
        mesh=mesh,
        in_specs=placed,
        out_specs=(P("row", None), P("lag", "row", None)),
        check_vma=False,
    )
```

```python
import functools

import jax
import jax.numpy as jnp
from jax import lax
from jax.experimental import pallas as pl
from jax.experimental.pallas import tpu as pltpu
from jax.sharding import PartitionSpec as P


STEPS = 3
AXES = ("lag", "row")


def broadcast(array, axis, root):
    mine = lax.axis_index(axis) == root
    return lax.psum(jnp.where(mine, array, jnp.zeros_like(array)), axis)


def from_behind(array, axis, by):
    length = lax.axis_size(axis)
    pairs = [(i, i + by) for i in range(length) if 0 <= i + by < length]
    return lax.ppermute(array, axis, pairs)


def plain_body(lag_ops, inverse, history, loads):
    acc = history
    local_lags = lag_ops.shape[0]
    local_rows = lag_ops.shape[1]
    total_cols = lag_ops.shape[2]
    loads_width = history.shape[2]
    flat_ops = lag_ops.reshape(local_lags * local_rows, total_cols)
    current = jnp.zeros((local_rows, loads_width), jnp.float32)
    for step in range(STEPS):
        rhs = broadcast(loads[step] - acc[0], "lag", 0)
        width = loads_width // lax.axis_size("lag")
        offset = lax.axis_index("lag") * width
        rhs_part = lax.dynamic_slice_in_dim(rhs, offset, width, 1)
        partial_value = jnp.dot(
            inverse,
            lax.all_gather(rhs_part, "row", axis=0, tiled=True),
            precision=lax.Precision.HIGHEST,
            preferred_element_type=jnp.float32,
        )
        current = lax.all_gather(partial_value, "lag", axis=1, tiled=True)
        product = jnp.dot(
            flat_ops,
            lax.all_gather(current, "row", axis=0, tiled=True),
            precision=lax.Precision.HIGHEST,
            preferred_element_type=jnp.float32,
        )
        product = product.reshape(local_lags, local_rows, loads_width)
        incoming = from_behind(acc[0], "lag", -1)
        shifted = jnp.concatenate([acc[1:], incoming[None]], axis=0)
        acc = shifted + product
    return (current, acc)


def swap(array, lag_bits, row_bits):
    lags, rows = lax.axis_size("lag"), lax.axis_size("row")
    pairs = [
        (g * rows + r, (g ^ lag_bits) * rows + (r ^ row_bits))
        for g in range(lags)
        for r in range(rows)
    ]
    return lax.ppermute(array, AXES, pairs)


def split(array):
    high = lax.reduce_precision(array, 8, 7)
    return high.astype(jnp.bfloat16), (array - high).astype(jnp.bfloat16)


def split_here(array):
    high = array.astype(jnp.bfloat16)
    return high, (array - high.astype(jnp.float32)).astype(jnp.bfloat16)


def contract(a, b):
    return lax.dot_general(
        a, b, (((1,), (1,)), ((), ())), preferred_element_type=jnp.float32
    )


def product(vector, matrix):
    vh, vl = vector
    mh, ml = matrix
    n = vh.shape[0]
    both = contract(jnp.concatenate([vh, vl], 0), mh)
    return both[:n] + both[n:] + contract(vh, ml)


def turn_first_kernel(history_ref, loads_ref, past_ref, rhs_ref):
    past_ref[...] = history_ref[0].T
    rhs_ref[...] = loads_ref[0].T - past_ref[...]


def turn_first(history, loads):
    _, rows, n = history.shape
    spec = pl.BlockSpec((1, rows, n), lambda i: (0, 0, 0))
    shape = jax.ShapeDtypeStruct((n, rows), history.dtype)
    out = pl.BlockSpec((n, rows), lambda i: (0, 0))
    return pl.pallas_call(
        turn_first_kernel,
        out_shape=(shape, shape),
        grid=(1,),
        in_specs=[spec, spec],
        out_specs=(out, out),
        compiler_params=pltpu.CompilerParams(vmem_limit_bytes=8 << 20),
        name="turn_first",
    )(history, loads)


def turn_kernel(history_ref, loads_ref, past_ref, given_ref):
    past_ref[...] = history_ref[1].T
    for i in range(given_ref.shape[0]):
        given_ref[i] = loads_ref[i + 1].T


def turn(history, loads):
    _, rows, n = history.shape
    return pl.pallas_call(
        turn_kernel,
        out_shape=(
            jax.ShapeDtypeStruct((n, rows), history.dtype),
            jax.ShapeDtypeStruct((loads.shape[0] - 1, n, rows), loads.dtype),
        ),
        compiler_params=pltpu.CompilerParams(vmem_limit_bytes=8 << 20),
        name="turn",
    )(history, loads)


def split_kernel(order_ref, m_ref, high_ref, low_ref):
    high_ref[...], low_ref[...] = split_here(m_ref[...])


def split_blocks(matrix, order, size, lag=None):
    rows, cols = matrix.shape[-2:]
    out = jax.ShapeDtypeStruct((rows, cols), jnp.bfloat16)
    spec = pl.BlockSpec((rows, size), lambda i, o: (0, i))
    if lag is None:
        source = pl.BlockSpec((rows, size), lambda i, o: (0, o[i]))
    else:
        source = pl.BlockSpec((None, rows, size), lambda i, o: (lag, 0, o[i]))
    return pl.pallas_call(
        split_kernel,
        out_shape=(out, out),
        grid_spec=pltpu.PrefetchScalarGridSpec(
            num_scalar_prefetch=1,
            grid=(cols // size,),
            in_specs=[source],
            out_specs=(spec, spec),
        ),
        compiler_params=pltpu.CompilerParams(vmem_limit_bytes=8 << 20),
        cost_estimate=pl.CostEstimate(
            flops=0, bytes_accessed=8 * rows * cols, transcendentals=0
        ),
        name="split_blocks",
    )(order, matrix)


VMEM = pl.BlockSpec(memory_space=pltpu.VMEM)


def times(vh, vl, high_ref, low_ref):
    n = vh.shape[0]
    both = contract(high_ref[...], jnp.concatenate([vh, vl], 0))
    return both[:, :n] + both[:, n:] + contract(low_ref[...], vh)


def field_kernel(step, high_ref, low_ref, v_ref, base_ref, *refs):
    total = base_ref[...] + times(*split_here(v_ref[...]), high_ref, low_ref).T
    if len(refs) == 1:
        refs[0][...] = total
    else:
        given_ref, out_ref, rhs_ref = refs
        out_ref[...] = total
        rhs_ref[...] = given_ref[step] - total


def costs(rows, cols, n):
    return pl.CostEstimate(
        flops=6 * rows * cols * n, bytes_accessed=4 * rows * cols, transcendentals=0
    )


def field(op, current, base, loads=None, step=0):
    high, low = op
    n = current.shape[0]
    shape = jax.ShapeDtypeStruct((n, high.shape[0]), jnp.float32)
    inputs = [high, low, current, base] + ([] if loads is None else [loads])
    return pl.pallas_call(
        functools.partial(field_kernel, step),
        out_shape=shape if loads is None else (shape, shape),
        in_specs=[VMEM] * len(inputs),
        out_specs=VMEM if loads is None else (VMEM, VMEM),
        compiler_params=pltpu.CompilerParams(vmem_limit_bytes=8 << 20),
        cost_estimate=costs(*high.shape, n),
        name="field",
    )(*inputs)


def last_kernel(h0_ref, l0_ref, h1_ref, l1_ref, v_ref, b0_ref, b1_ref, current_ref, out_ref):
    rows = current_ref.shape[0]
    vh, vl = split_here(v_ref[...])
    current_ref[...] = v_ref[:, :rows].T
    out_ref[0] = b0_ref[...].T + times(vh, vl, h0_ref, l0_ref)
    out_ref[1] = b1_ref[...].T + times(vh, vl, h1_ref, l1_ref)


def last(op0, op1, current, base0, base1):
    rows, cols = op0[0].shape
    n = current.shape[0]
    return pl.pallas_call(
        last_kernel,
        out_shape=(
            jax.ShapeDtypeStruct((rows, n), jnp.float32),
            jax.ShapeDtypeStruct((2, rows, n), jnp.float32),
        ),
        in_specs=[VMEM] * 7,
        out_specs=(VMEM, VMEM),
        compiler_params=pltpu.CompilerParams(vmem_limit_bytes=8 << 20),
        cost_estimate=costs(2 * rows, cols, n),
        name="last",
    )(*op0, *op1, current, base0, base1)


def quad_body(lag_ops, inverse, history, loads):
    rows_n = lax.axis_size("row")
    height = lag_ops.shape[1]
    width = loads.shape[2] // 4
    g = lax.axis_index("lag")
    r = lax.axis_index("row")
    plane, core = g // 2, g % 2
    near = [k for k in range(0, rows_n, 2)]
    steps = near + [k + 1 for k in near]
    cut = len(near) * height
    order = r ^ jnp.array(steps, jnp.int32)

    def line(v):
        return jnp.concatenate([v] + [swap(v, 0, k) for k in near[1:]], 1)

    def scatter(rhs):
        parts = [rhs[j * width : (j + 1) * width] for j in range(4)]
        got = [parts[0]] + [swap(parts[j], j, 0) for j in (3, 2, 1)][::-1]
        return lax.select_n(g, *got)

    def full(a):
        near_y, far_y, far = swap(a, 2, 0), swap(a, 2, 1), swap(a, 0, 1)
        near_ = jnp.concatenate([a, near_y], 0)
        far_ = jnp.concatenate([far, far_y], 0)
        v = jnp.concatenate([near_, far_], 1)
        w = jnp.concatenate([swap(near_, 1, 0), swap(far_, 1, 0)], 1)
        chunks = [v[:width], w[:width], v[width:], w[width:]]
        even = [jnp.where(core == 0, chunks[j], chunks[j ^ 1]) for j in range(4)]
        return jnp.concatenate(
            [jnp.where(plane == 0, even[j], even[j ^ 2]) for j in range(4)], 0
        )

    def behind(array):
        near_, far = swap(array, 1, 0), swap(array, 3, 0)
        return jnp.where(core == 0, near_, jnp.where(plane == 0, far, 0.0))

    tie = lax.optimization_barrier
    keep = functools.partial(pltpu.with_memory_space_constraint, memory_space=pltpu.HBM)
    acc0, rhs = turn_first(keep(history), keep(loads))
    for step in range(STEPS):
        rhs = scatter(rhs)
        if step == 0:
            rhs, inverse = tie((rhs, inverse))
            high, low = split_blocks(inverse, order, height)
            inv = [(high[:, :cut], low[:, :cut]), (high[:, cut:], low[:, cut:])]
            a = line(rhs)
            a, inv = tie((a, inv))
            a, acc0, ops0, history, loads = tie((a, acc0, lag_ops, history, loads))
            acc1, given = turn(history, loads)
            op0 = split_blocks(ops0, order, height, 0)
            b = swap(a, 0, 1)
            b, acc1, given, op0 = tie((b, acc1, given, op0))
        else:
            a = line(rhs)
            a, acc0, current = tie((a, acc0, current))
            acc1 = field(op1, current, below)
            b = swap(a, 0, 1)
            b, acc1 = tie((b, acc1))
        ahead = behind(acc0)
        solved = product(split(a), inv[0]) + product(split(b), inv[1])
        if step == 0:
            solved, ops1 = tie((solved, lag_ops))
            op1 = split_blocks(ops1, order, height, 1)
        a = line(solved)
        a, op1 = tie((a, op1))
        current = full(a)
        below = ahead
        if step < STEPS - 1:
            acc0, rhs = field(op0, current, acc1, given, step)
    return last(op0, op1, current, acc1, below)


def solution(mesh):
    placed = (P("lag", "row", None), P("row", None), P("lag", "row", None), P(None, "row", None))

    def body(lag_ops, inverse, history, loads):
        lags, rows = lax.axis_size("lag"), lax.axis_size("row")
        fits = (
            lags == 4
            and lag_ops.shape[0] == STEPS - 1
            and rows & (rows - 1) == 0
            and lag_ops.shape[1] * rows == lag_ops.shape[2]
            and loads.shape[0] == STEPS
        )
        return (quad_body if fits else plain_body)(lag_ops, inverse, history, loads)

    return jax.shard_map(
        body,
        mesh=mesh,
        in_specs=placed,
        out_specs=(P("row", None), P("lag", "row", None)),
        check_vma=False,
    )
```

```python
import functools

import jax
import jax.numpy as jnp
from jax import lax
from jax.experimental import pallas as pl
from jax.experimental.pallas import tpu as pltpu
from jax.sharding import PartitionSpec as P


STEPS = 3
AXES = ("lag", "row")


def broadcast(array, axis, root):
    mine = lax.axis_index(axis) == root
    return lax.psum(jnp.where(mine, array, jnp.zeros_like(array)), axis)


def from_behind(array, axis, by):
    length = lax.axis_size(axis)
    pairs = [(i, i + by) for i in range(length) if 0 <= i + by < length]
    return lax.ppermute(array, axis, pairs)


def plain_body(lag_ops, inverse, history, loads):
    acc = history
    local_lags = lag_ops.shape[0]
    local_rows = lag_ops.shape[1]
    total_cols = lag_ops.shape[2]
    loads_width = history.shape[2]
    flat_ops = lag_ops.reshape(local_lags * local_rows, total_cols)
    current = jnp.zeros((local_rows, loads_width), jnp.float32)
    for step in range(STEPS):
        rhs = broadcast(loads[step] - acc[0], "lag", 0)
        width = loads_width // lax.axis_size("lag")
        offset = lax.axis_index("lag") * width
        rhs_part = lax.dynamic_slice_in_dim(rhs, offset, width, 1)
        partial_value = jnp.dot(
            inverse,
            lax.all_gather(rhs_part, "row", axis=0, tiled=True),
            precision=lax.Precision.HIGHEST,
            preferred_element_type=jnp.float32,
        )
        current = lax.all_gather(partial_value, "lag", axis=1, tiled=True)
        product = jnp.dot(
            flat_ops,
            lax.all_gather(current, "row", axis=0, tiled=True),
            precision=lax.Precision.HIGHEST,
            preferred_element_type=jnp.float32,
        )
        product = product.reshape(local_lags, local_rows, loads_width)
        incoming = from_behind(acc[0], "lag", -1)
        shifted = jnp.concatenate([acc[1:], incoming[None]], axis=0)
        acc = shifted + product
    return (current, acc)


def swap(array, lag_bits, row_bits):
    lags, rows = lax.axis_size("lag"), lax.axis_size("row")
    pairs = [
        (g * rows + r, (g ^ lag_bits) * rows + (r ^ row_bits))
        for g in range(lags)
        for r in range(rows)
    ]
    return lax.ppermute(array, AXES, pairs)


def split(array):
    high = lax.reduce_precision(array, 8, 7)
    return high.astype(jnp.bfloat16), (array - high).astype(jnp.bfloat16)


def split_here(array):
    high = array.astype(jnp.bfloat16)
    return high, (array - high.astype(jnp.float32)).astype(jnp.bfloat16)


def contract(a, b):
    return lax.dot_general(
        a, b, (((1,), (1,)), ((), ())), preferred_element_type=jnp.float32
    )


def product(vector, matrix):
    vh, vl = vector
    mh, ml = matrix
    n = vh.shape[0]
    both = contract(jnp.concatenate([vh, vl], 0), mh)
    return both[:n] + both[n:] + contract(vh, ml)


def turn_first_kernel(history_ref, loads_ref, past_ref, rhs_ref):
    past_ref[...] = history_ref[0].T
    rhs_ref[...] = loads_ref[0].T - past_ref[...]


def turn_first(history, loads):
    _, rows, n = history.shape
    spec = pl.BlockSpec((1, rows, n), lambda i: (0, 0, 0))
    shape = jax.ShapeDtypeStruct((n, rows), history.dtype)
    out = pl.BlockSpec((n, rows), lambda i: (0, 0))
    return pl.pallas_call(
        turn_first_kernel,
        out_shape=(shape, shape),
        grid=(1,),
        in_specs=[spec, spec],
        out_specs=(out, out),
        compiler_params=pltpu.CompilerParams(vmem_limit_bytes=8 << 20),
        name="turn_first",
    )(history, loads)


def turn_kernel(history_ref, loads_ref, past_ref, given_ref):
    past_ref[...] = history_ref[1].T
    for i in range(given_ref.shape[0]):
        given_ref[i] = loads_ref[i + 1].T


def turn(history, loads):
    _, rows, n = history.shape
    return pl.pallas_call(
        turn_kernel,
        out_shape=(
            jax.ShapeDtypeStruct((n, rows), history.dtype),
            jax.ShapeDtypeStruct((loads.shape[0] - 1, n, rows), loads.dtype),
        ),
        compiler_params=pltpu.CompilerParams(vmem_limit_bytes=8 << 20),
        name="turn",
    )(history, loads)


def split_kernel(order_ref, m_ref, high_ref, low_ref):
    high_ref[...], low_ref[...] = split_here(m_ref[...])


def split_blocks(matrix, order, size, lag=None):
    rows, cols = matrix.shape[-2:]
    out = jax.ShapeDtypeStruct((rows, cols), jnp.bfloat16)
    spec = pl.BlockSpec((rows, size), lambda i, o: (0, i))
    if lag is None:
        source = pl.BlockSpec((rows, size), lambda i, o: (0, o[i]))
    else:
        source = pl.BlockSpec((None, rows, size), lambda i, o: (lag, 0, o[i]))
    return pl.pallas_call(
        split_kernel,
        out_shape=(out, out),
        grid_spec=pltpu.PrefetchScalarGridSpec(
            num_scalar_prefetch=1,
            grid=(cols // size,),
            in_specs=[source],
            out_specs=(spec, spec),
        ),
        compiler_params=pltpu.CompilerParams(vmem_limit_bytes=8 << 20),
        cost_estimate=pl.CostEstimate(
            flops=0, bytes_accessed=8 * rows * cols, transcendentals=0
        ),
        name="split_blocks",
    )(order, matrix)


VMEM = pl.BlockSpec(memory_space=pltpu.VMEM)


def times(vh, vl, high_ref, low_ref):
    n = vh.shape[0]
    both = contract(high_ref[...], jnp.concatenate([vh, vl], 0))
    return both[:, :n] + both[:, n:] + contract(low_ref[...], vh)


def field_kernel(step, high_ref, low_ref, v_ref, base_ref, *refs):
    total = base_ref[...] + times(*split_here(v_ref[...]), high_ref, low_ref).T
    if len(refs) == 1:
        refs[0][...] = total
    else:
        given_ref, out_ref, rhs_ref = refs
        out_ref[...] = total
        rhs_ref[...] = given_ref[step] - total


def costs(rows, cols, n):
    return pl.CostEstimate(
        flops=6 * rows * cols * n, bytes_accessed=4 * rows * cols, transcendentals=0
    )


def field(op, current, base, loads=None, step=0):
    high, low = op
    n = current.shape[0]
    shape = jax.ShapeDtypeStruct((n, high.shape[0]), jnp.float32)
    inputs = [high, low, current, base] + ([] if loads is None else [loads])
    return pl.pallas_call(
        functools.partial(field_kernel, step),
        out_shape=shape if loads is None else (shape, shape),
        in_specs=[VMEM] * len(inputs),
        out_specs=VMEM if loads is None else (VMEM, VMEM),
        compiler_params=pltpu.CompilerParams(vmem_limit_bytes=8 << 20),
        cost_estimate=costs(*high.shape, n),
        name="field",
    )(*inputs)


def last_kernel(h0_ref, l0_ref, h1_ref, l1_ref, v_ref, b0_ref, b1_ref, current_ref, out_ref):
    rows = current_ref.shape[0]
    vh, vl = split_here(v_ref[...])
    current_ref[...] = v_ref[:, :rows].T
    out_ref[0] = b0_ref[...].T + times(vh, vl, h0_ref, l0_ref)
    out_ref[1] = b1_ref[...].T + times(vh, vl, h1_ref, l1_ref)


def last(op0, op1, current, base0, base1):
    rows, cols = op0[0].shape
    n = current.shape[0]
    return pl.pallas_call(
        last_kernel,
        out_shape=(
            jax.ShapeDtypeStruct((rows, n), jnp.float32),
            jax.ShapeDtypeStruct((2, rows, n), jnp.float32),
        ),
        in_specs=[VMEM] * 7,
        out_specs=(VMEM, VMEM),
        compiler_params=pltpu.CompilerParams(vmem_limit_bytes=8 << 20),
        cost_estimate=costs(2 * rows, cols, n),
        name="last",
    )(*op0, *op1, current, base0, base1)


def quad_body(lag_ops, inverse, history, loads):
    rows_n = lax.axis_size("row")
    height = lag_ops.shape[1]
    width = loads.shape[2] // 4
    g = lax.axis_index("lag")
    r = lax.axis_index("row")
    first_plane, first_core = g < 2, (g & 1) == 0
    near = [k for k in range(0, rows_n, 2)]
    steps = near + [k + 1 for k in near]
    cut = len(near) * height
    order = r ^ jnp.array(steps, jnp.int32)

    def line(v):
        return jnp.concatenate([v] + [swap(v, 0, k) for k in near[1:]], 1)

    def scatter(rhs):
        parts = [rhs[j * width : (j + 1) * width] for j in range(4)]
        got = [parts[0]] + [swap(parts[j], j, 0) for j in (3, 2, 1)][::-1]
        return lax.select_n(g, *got)

    def full(a):
        near_y, far_y, far = swap(a, 2, 0), swap(a, 2, 1), swap(a, 0, 1)
        near_ = jnp.concatenate([a, near_y], 0)
        far_ = jnp.concatenate([far, far_y], 0)
        v = jnp.concatenate([near_, far_], 1)
        w = jnp.concatenate([swap(near_, 1, 0), swap(far_, 1, 0)], 1)
        chunks = [v[:width], w[:width], v[width:], w[width:]]
        even = [jnp.where(first_core, chunks[j], chunks[j ^ 1]) for j in range(4)]
        return jnp.concatenate(
            [jnp.where(first_plane, even[j], even[j ^ 2]) for j in range(4)], 0
        )

    def behind(array):
        near_, far = swap(array, 1, 0), swap(array, 3, 0)
        return jnp.where(first_core, near_, jnp.where(first_plane, far, 0.0))

    tie = lax.optimization_barrier
    keep = functools.partial(pltpu.with_memory_space_constraint, memory_space=pltpu.HBM)
    acc0, rhs = turn_first(keep(history), keep(loads))
    rhs, first_plane, first_core, g, order = tie((rhs, first_plane, first_core, g, order))
    for step in range(STEPS):
        rhs = scatter(rhs)
        if step == 0:
            rhs, order = tie((rhs, order))
            high, low = split_blocks(inverse, order, height)
            inv = [(high[:, :cut], low[:, :cut]), (high[:, cut:], low[:, cut:])]
            a = line(rhs)
            a, inv = tie((a, inv))
            a, acc0, order = tie((a, acc0, order))
            acc1, given = turn(history, loads)
            op0 = split_blocks(lag_ops, order, height, 0)
            b = swap(a, 0, 1)
            b, acc1, given, op0 = tie((b, acc1, given, op0))
        else:
            a = line(rhs)
            a, acc0, current = tie((a, acc0, current))
            acc1 = field(op1, current, below)
            b = swap(a, 0, 1)
            b, acc1 = tie((b, acc1))
        ahead = behind(acc0)
        solved = product(split(a), inv[0]) + product(split(b), inv[1])
        if step == 0:
            solved, order = tie((solved, order))
            op1 = split_blocks(lag_ops, order, height, 1)
        a = line(solved)
        a, op1 = tie((a, op1))
        current = full(a)
        below = ahead
        if step < STEPS - 1:
            acc0, rhs = field(op0, current, acc1, given, step)
    return last(op0, op1, current, acc1, below)


def solution(mesh):
    placed = (P("lag", "row", None), P("row", None), P("lag", "row", None), P(None, "row", None))

    def body(lag_ops, inverse, history, loads):
        lags, rows = lax.axis_size("lag"), lax.axis_size("row")
        fits = (
            lags == 4
            and lag_ops.shape[0] == STEPS - 1
            and rows & (rows - 1) == 0
            and lag_ops.shape[1] * rows == lag_ops.shape[2]
            and loads.shape[0] == STEPS
        )
        return (quad_body if fits else plain_body)(lag_ops, inverse, history, loads)

    return jax.shard_map(
        body,
        mesh=mesh,
        in_specs=placed,
        out_specs=(P("row", None), P("lag", "row", None)),
        check_vma=False,
    )
```

```python
import functools

import jax
import jax.numpy as jnp
from jax import lax
from jax.experimental import pallas as pl
from jax.experimental.pallas import tpu as pltpu
from jax.sharding import PartitionSpec as P


STEPS = 3
AXES = ("lag", "row")


def broadcast(array, axis, root):
    mine = lax.axis_index(axis) == root
    return lax.psum(jnp.where(mine, array, jnp.zeros_like(array)), axis)


def from_behind(array, axis, by):
    length = lax.axis_size(axis)
    pairs = [(i, i + by) for i in range(length) if 0 <= i + by < length]
    return lax.ppermute(array, axis, pairs)


def plain_body(lag_ops, inverse, history, loads):
    acc = history
    local_lags = lag_ops.shape[0]
    local_rows = lag_ops.shape[1]
    total_cols = lag_ops.shape[2]
    loads_width = history.shape[2]
    flat_ops = lag_ops.reshape(local_lags * local_rows, total_cols)
    current = jnp.zeros((local_rows, loads_width), jnp.float32)
    for step in range(STEPS):
        rhs = broadcast(loads[step] - acc[0], "lag", 0)
        width = loads_width // lax.axis_size("lag")
        offset = lax.axis_index("lag") * width
        rhs_part = lax.dynamic_slice_in_dim(rhs, offset, width, 1)
        partial_value = jnp.dot(
            inverse,
            lax.all_gather(rhs_part, "row", axis=0, tiled=True),
            precision=lax.Precision.HIGHEST,
            preferred_element_type=jnp.float32,
        )
        current = lax.all_gather(partial_value, "lag", axis=1, tiled=True)
        product = jnp.dot(
            flat_ops,
            lax.all_gather(current, "row", axis=0, tiled=True),
            precision=lax.Precision.HIGHEST,
            preferred_element_type=jnp.float32,
        )
        product = product.reshape(local_lags, local_rows, loads_width)
        incoming = from_behind(acc[0], "lag", -1)
        shifted = jnp.concatenate([acc[1:], incoming[None]], axis=0)
        acc = shifted + product
    return (current, acc)


def swap(array, lag_bits, row_bits):
    lags, rows = lax.axis_size("lag"), lax.axis_size("row")
    pairs = [
        (g * rows + r, (g ^ lag_bits) * rows + (r ^ row_bits))
        for g in range(lags)
        for r in range(rows)
    ]
    return lax.ppermute(array, AXES, pairs)


def split(array):
    high = lax.reduce_precision(array, 8, 7)
    return high.astype(jnp.bfloat16), (array - high).astype(jnp.bfloat16)


def split_here(array):
    high = array.astype(jnp.bfloat16)
    return high, (array - high.astype(jnp.float32)).astype(jnp.bfloat16)


def contract(a, b):
    return lax.dot_general(
        a, b, (((1,), (1,)), ((), ())), preferred_element_type=jnp.float32
    )


def product(vector, matrix):
    vh, vl = vector
    mh, ml = matrix
    n = vh.shape[0]
    both = contract(jnp.concatenate([vh, vl], 0), mh)
    return both[:n] + both[n:] + contract(vh, ml)


VMEM = pl.BlockSpec(memory_space=pltpu.VMEM)
SMEM = pl.BlockSpec(memory_space=pltpu.SMEM)


def turn_first_kernel(history_ref, loads_ref, past_ref, rhs_ref):
    past_ref[...] = history_ref[0].T
    rhs_ref[...] = loads_ref[0].T - past_ref[...]


def turn_first(history, loads):
    _, rows, n = history.shape
    spec = pl.BlockSpec((1, rows, n), lambda i: (0, 0, 0))
    shape = jax.ShapeDtypeStruct((n, rows), history.dtype)
    out = pl.BlockSpec((n, rows), lambda i: (0, 0))
    return pl.pallas_call(
        turn_first_kernel,
        out_shape=(shape, shape),
        grid=(1,),
        in_specs=[spec, spec],
        out_specs=(out, out),
        compiler_params=pltpu.CompilerParams(vmem_limit_bytes=8 << 20),
        name="turn_first",
    )(history, loads)


def turn_kernel(history_ref, loads_ref, past_ref, given_ref):
    past_ref[...] = history_ref[1].T
    for i in range(given_ref.shape[0]):
        given_ref[i] = loads_ref[i + 1].T


def turn(history, loads):
    _, rows, n = history.shape
    return pl.pallas_call(
        turn_kernel,
        out_shape=(
            jax.ShapeDtypeStruct((n, rows), history.dtype),
            jax.ShapeDtypeStruct((loads.shape[0] - 1, n, rows), loads.dtype),
        ),
        compiler_params=pltpu.CompilerParams(vmem_limit_bytes=8 << 20),
        name="turn",
    )(history, loads)


def split_kernel(lag, picks, order_ref, *refs):
    high_ref, low_ref, buffer, arrived = refs[-4:]
    size = buffer.shape[1] // order_ref.shape[0]

    def copies(source_ref):
        view = source_ref if lag is None else source_ref.at[lag]
        return [
            pltpu.make_async_copy(
                view.at[:, pl.ds(pl.multiple_of(order_ref[i] * size, 128), size)],
                buffer.at[:, pl.ds(i * size, size)],
                arrived.at[i],
            )
            for i in range(order_ref.shape[0])
        ]

    if picks:
        pick_ref, first_ref, second_ref = refs[:3]

        @pl.when(pick_ref[0] == 0)
        def _():
            for copy in copies(first_ref):
                copy.start()

        @pl.when(pick_ref[0] != 0)
        def _():
            for copy in copies(second_ref):
                copy.start()
    else:
        first_ref = refs[0]
        for copy in copies(first_ref):
            copy.start()
    for i, copy in enumerate(copies(first_ref)):
        copy.wait()
        part = pl.ds(i * size, size)
        high_ref[:, part], low_ref[:, part] = split_here(buffer[:, part])


def split_blocks(matrix, order, lag=None, pick=None, other=None):
    rows, cols = matrix.shape[-2:]
    out = jax.ShapeDtypeStruct((rows, cols), jnp.bfloat16)
    inputs, specs = [order], [SMEM]
    if pick is not None:
        inputs, specs = inputs + [pick], specs + [SMEM]
    sources = [matrix] if other is None else [matrix, other]
    return pl.pallas_call(
        functools.partial(split_kernel, lag, pick is not None),
        out_shape=(out, out),
        in_specs=specs + [pl.BlockSpec(memory_space=pltpu.HBM)] * len(sources),
        out_specs=(VMEM, VMEM),
        scratch_shapes=[
            pltpu.VMEM((rows, cols), jnp.float32),
            pltpu.SemaphoreType.DMA((order.shape[0],)),
        ],
        compiler_params=pltpu.CompilerParams(vmem_limit_bytes=8 << 20),
        cost_estimate=pl.CostEstimate(
            flops=0, bytes_accessed=8 * rows * cols, transcendentals=0
        ),
        name="split_blocks",
    )(*inputs, *sources)


def times(vh, vl, high_ref, low_ref):
    n = vh.shape[0]
    both = contract(high_ref[...], jnp.concatenate([vh, vl], 0))
    return both[:, :n] + both[:, n:] + contract(low_ref[...], vh)


def field_kernel(high_ref, low_ref, v_ref, base_ref, out_ref):
    out_ref[...] = base_ref[...] + times(*split_here(v_ref[...]), high_ref, low_ref).T


def costs(rows, cols, n):
    return pl.CostEstimate(
        flops=6 * rows * cols * n, bytes_accessed=4 * rows * cols, transcendentals=0
    )


def field(op, current, base):
    high, low = op
    n = current.shape[0]
    return pl.pallas_call(
        field_kernel,
        out_shape=jax.ShapeDtypeStruct((n, high.shape[0]), jnp.float32),
        in_specs=[VMEM] * 4,
        out_specs=VMEM,
        compiler_params=pltpu.CompilerParams(vmem_limit_bytes=8 << 20),
        cost_estimate=costs(*high.shape, n),
        name="field",
    )(high, low, current, base)


def lead_kernel(high_ref, low_ref, near_ref, far_ref, rest_ref, mine_ref, theirs_ref):
    v = jnp.concatenate([near_ref[...], far_ref[...]], 1)
    rhs = rest_ref[...] - times(*split_here(v), high_ref, low_ref).T
    n = mine_ref.shape[0]
    mine_ref[...] = rhs[:n]
    theirs_ref[...] = rhs[n:]


def lead(op, near, far, rest):
    high, low = op
    n = near.shape[0]
    shape = jax.ShapeDtypeStruct((n // 2, high.shape[0]), jnp.float32)
    return pl.pallas_call(
        lead_kernel,
        out_shape=(shape, shape),
        in_specs=[VMEM] * 5,
        out_specs=(VMEM, VMEM),
        compiler_params=pltpu.CompilerParams(vmem_limit_bytes=8 << 20),
        cost_estimate=costs(*high.shape, n),
        name="lead",
    )(high, low, near, far, rest)


def last_kernel(h0_ref, l0_ref, h1_ref, l1_ref, v_ref, b0_ref, b1_ref, current_ref, out_ref):
    rows = current_ref.shape[0]
    vh, vl = split_here(v_ref[...])
    current_ref[...] = v_ref[:, :rows].T
    out_ref[0] = b0_ref[...].T + times(vh, vl, h0_ref, l0_ref)
    out_ref[1] = b1_ref[...].T + times(vh, vl, h1_ref, l1_ref)


def last(op0, op1, current, base0, base1):
    rows, cols = op0[0].shape
    n = current.shape[0]
    return pl.pallas_call(
        last_kernel,
        out_shape=(
            jax.ShapeDtypeStruct((rows, n), jnp.float32),
            jax.ShapeDtypeStruct((2, rows, n), jnp.float32),
        ),
        in_specs=[VMEM] * 7,
        out_specs=(VMEM, VMEM),
        compiler_params=pltpu.CompilerParams(vmem_limit_bytes=8 << 20),
        cost_estimate=costs(2 * rows, cols, n),
        name="last",
    )(*op0, *op1, current, base0, base1)


def quad_body(lag_ops, inverse, history, loads):
    rows_n = lax.axis_size("row")
    height = lag_ops.shape[1]
    width = loads.shape[2] // 4
    g = lax.axis_index("lag")
    r = lax.axis_index("row")
    first_plane, first_core = g < 2, (g & 1) == 0
    near = [k for k in range(0, rows_n, 2)]
    steps = near + [k + 1 for k in near]
    cut = len(near) * height
    order = r ^ jnp.array(steps, jnp.int32)

    def line(v):
        return jnp.concatenate([v] + [swap(v, 0, k) for k in near[1:]], 1)

    def scatter(rhs):
        parts = [rhs[j * width : (j + 1) * width] for j in range(4)]
        got = [parts[0]] + [swap(parts[j], j, 0) for j in (3, 2, 1)][::-1]
        return lax.select_n(g, *got)

    def exchange(a):
        near_y, far_y, far = swap(a, 2, 0), swap(a, 2, 1), swap(a, 0, 1)
        return jnp.concatenate([a, near_y], 0), jnp.concatenate([far, far_y], 0)

    def full(near_, far_):
        v = jnp.concatenate([near_, far_], 1)
        w = jnp.concatenate([swap(near_, 1, 0), swap(far_, 1, 0)], 1)
        chunks = [v[:width], w[:width], v[width:], w[width:]]
        even = [jnp.where(first_core, chunks[j], chunks[j ^ 1]) for j in range(4)]
        return jnp.concatenate(
            [jnp.where(first_plane, even[j], even[j ^ 2]) for j in range(4)], 0
        )

    def behind(array):
        return swap(array, 1, 0), swap(array, 3, 0)

    def choose(received):
        near_, far = received
        return jnp.where(first_core, near_, jnp.where(first_plane, far, 0.0))

    def pick(array, j):
        return jnp.concatenate([array[(j + k) * width : (j + k + 1) * width] for k in (0, 2)], 0)

    def pair(array):
        return jnp.where(first_core, pick(array, 0), swap(pick(array, 1), 1, 0))

    tie = lax.optimization_barrier
    keep = functools.partial(pltpu.with_memory_space_constraint, memory_space=pltpu.HBM)
    acc0, rhs = turn_first(keep(history), keep(loads))
    rhs, first_plane, first_core, g = tie((rhs, first_plane, first_core, g))
    which = (g & 1).reshape(1)
    rhs = scatter(rhs)
    rhs, acc0, sent_ops = tie((rhs, acc0, lag_ops))
    other_ops = swap(sent_ops, 1, 0)
    for step in range(STEPS):
        if step == 0:
            rhs, order, which = tie((rhs, order, which))
            high, low = split_blocks(keep(inverse), order)
            inv = [(high[:, :cut], low[:, :cut]), (high[:, cut:], low[:, cut:])]
            a = line(rhs)
            a, inv = tie((a, inv))
            acc1, given = turn(history, loads)
            b = swap(a, 0, 1)
            b, acc1, given = tie((b, acc1, given))
        else:
            current = full(near_, far_)
            rhs, current, received = tie((rhs, current, received))
            below = choose(received)
            new0 = field(own0, current, acc1)
            a = line(rhs)
            a, acc0, current = tie((a, new0, current))
            acc1 = field(own1, current, below)
            b = swap(a, 0, 1)
            b, acc1 = tie((b, acc1))
        received = behind(acc0)
        solved = product(split(a), inv[0]) + product(split(b), inv[1])
        if step == 0:
            solved, order, which = tie((solved, order, which))
            first = split_blocks(keep(lag_ops), order, 0, which, keep(other_ops))
        a = line(solved)
        if step < STEPS - 1:
            led = pair(acc1)
            rest = jnp.where(first_core, pick(given[step], 0), pick(given[step], 1)) - led
        if step == 0:
            a, first, order = tie((a, first, order))
            own0 = split_blocks(keep(lag_ops), order, 0)
            own1 = split_blocks(keep(lag_ops), order, 1)
        near_, far_ = exchange(a)
        if step == 0:
            near_, far_, own0, own1 = tie((near_, far_, own0, own1))
        if step < STEPS - 1:
            near_, far_, rest = tie((near_, far_, rest))
            mine, theirs = lead(first, near_, far_, rest)
            rhs = jnp.where(first_plane, mine, swap(theirs, 2, 0))
    current = full(near_, far_)
    return last(own0, own1, current, acc1, choose(received))


def solution(mesh):
    placed = (P("lag", "row", None), P("row", None), P("lag", "row", None), P(None, "row", None))

    def body(lag_ops, inverse, history, loads):
        lags, rows = lax.axis_size("lag"), lax.axis_size("row")
        fits = (
            lags == 4
            and lag_ops.shape[0] == STEPS - 1
            and rows & (rows - 1) == 0
            and lag_ops.shape[1] * rows == lag_ops.shape[2]
            and loads.shape[0] == STEPS
        )
        return (quad_body if fits else plain_body)(lag_ops, inverse, history, loads)

    return jax.shard_map(
        body,
        mesh=mesh,
        in_specs=placed,
        out_specs=(P("row", None), P("lag", "row", None)),
        check_vma=False,
    )
```

```python
import functools

import jax
import jax.numpy as jnp
from jax import lax
from jax.experimental import pallas as pl
from jax.experimental.pallas import tpu as pltpu
from jax.sharding import PartitionSpec as P


STEPS = 3
AXES = ("lag", "row")


def broadcast(array, axis, root):
    mine = lax.axis_index(axis) == root
    return lax.psum(jnp.where(mine, array, jnp.zeros_like(array)), axis)


def from_behind(array, axis, by):
    length = lax.axis_size(axis)
    pairs = [(i, i + by) for i in range(length) if 0 <= i + by < length]
    return lax.ppermute(array, axis, pairs)


def plain_body(lag_ops, inverse, history, loads):
    acc = history
    local_lags = lag_ops.shape[0]
    local_rows = lag_ops.shape[1]
    total_cols = lag_ops.shape[2]
    loads_width = history.shape[2]
    flat_ops = lag_ops.reshape(local_lags * local_rows, total_cols)
    current = jnp.zeros((local_rows, loads_width), jnp.float32)
    for step in range(STEPS):
        rhs = broadcast(loads[step] - acc[0], "lag", 0)
        width = loads_width // lax.axis_size("lag")
        offset = lax.axis_index("lag") * width
        rhs_part = lax.dynamic_slice_in_dim(rhs, offset, width, 1)
        partial_value = jnp.dot(
            inverse,
            lax.all_gather(rhs_part, "row", axis=0, tiled=True),
            precision=lax.Precision.HIGHEST,
            preferred_element_type=jnp.float32,
        )
        current = lax.all_gather(partial_value, "lag", axis=1, tiled=True)
        product = jnp.dot(
            flat_ops,
            lax.all_gather(current, "row", axis=0, tiled=True),
            precision=lax.Precision.HIGHEST,
            preferred_element_type=jnp.float32,
        )
        product = product.reshape(local_lags, local_rows, loads_width)
        incoming = from_behind(acc[0], "lag", -1)
        shifted = jnp.concatenate([acc[1:], incoming[None]], axis=0)
        acc = shifted + product
    return (current, acc)


def swap(array, lag_bits, row_bits):
    lags, rows = lax.axis_size("lag"), lax.axis_size("row")
    pairs = [
        (g * rows + r, (g ^ lag_bits) * rows + (r ^ row_bits))
        for g in range(lags)
        for r in range(rows)
    ]
    return lax.ppermute(array, AXES, pairs)


def split(array):
    high = lax.reduce_precision(array, 8, 7)
    return high.astype(jnp.bfloat16), (array - high).astype(jnp.bfloat16)


def split_here(array):
    high = array.astype(jnp.bfloat16)
    return high, (array - high.astype(jnp.float32)).astype(jnp.bfloat16)


def contract(a, b):
    return lax.dot_general(
        a, b, (((1,), (1,)), ((), ())), preferred_element_type=jnp.float32
    )


def product(vector, matrix):
    vh, vl = vector
    mh, ml = matrix
    n = vh.shape[0]
    both = contract(jnp.concatenate([vh, vl], 0), mh)
    return both[:n] + both[n:] + contract(vh, ml)


VMEM = pl.BlockSpec(memory_space=pltpu.VMEM)
SMEM = pl.BlockSpec(memory_space=pltpu.SMEM)


def turn_first_kernel(history_ref, loads_ref, past_ref, rhs_ref):
    past_ref[...] = history_ref[0].T
    rhs_ref[...] = loads_ref[0].T - past_ref[...]


def turn_first(history, loads):
    _, rows, n = history.shape
    spec = pl.BlockSpec((1, rows, n), lambda i: (0, 0, 0))
    shape = jax.ShapeDtypeStruct((n, rows), history.dtype)
    out = pl.BlockSpec((n, rows), lambda i: (0, 0))
    return pl.pallas_call(
        turn_first_kernel,
        out_shape=(shape, shape),
        grid=(1,),
        in_specs=[spec, spec],
        out_specs=(out, out),
        compiler_params=pltpu.CompilerParams(vmem_limit_bytes=8 << 20),
        name="turn_first",
    )(history, loads)


def turn_kernel(history_ref, loads_ref, past_ref, given_ref):
    past_ref[...] = history_ref[1].T
    for i in range(given_ref.shape[0]):
        given_ref[i] = loads_ref[i + 1].T


def turn(history, loads):
    _, rows, n = history.shape
    return pl.pallas_call(
        turn_kernel,
        out_shape=(
            jax.ShapeDtypeStruct((n, rows), history.dtype),
            jax.ShapeDtypeStruct((loads.shape[0] - 1, n, rows), loads.dtype),
        ),
        compiler_params=pltpu.CompilerParams(vmem_limit_bytes=8 << 20),
        name="turn",
    )(history, loads)


def split_kernel(lag, picks, order_ref, *refs):
    high_ref, low_ref, buffer, arrived = refs[-4:]
    size = buffer.shape[1] // order_ref.shape[0]

    def copies(source_ref):
        view = source_ref if lag is None else source_ref.at[lag]
        return [
            pltpu.make_async_copy(
                view.at[:, pl.ds(pl.multiple_of(order_ref[i] * size, 128), size)],
                buffer.at[:, pl.ds(i * size, size)],
                arrived.at[i],
            )
            for i in range(order_ref.shape[0])
        ]

    if picks:
        pick_ref, first_ref, second_ref = refs[:3]

        @pl.when(pick_ref[0] == 0)
        def _():
            for copy in copies(first_ref):
                copy.start()

        @pl.when(pick_ref[0] != 0)
        def _():
            for copy in copies(second_ref):
                copy.start()
    else:
        first_ref = refs[0]
        for copy in copies(first_ref):
            copy.start()
    for i, copy in enumerate(copies(first_ref)):
        copy.wait()
        part = pl.ds(i * size, size)
        high_ref[:, part], low_ref[:, part] = split_here(buffer[:, part])


def split_blocks(matrix, order, lag=None, pick=None, other=None):
    rows, cols = matrix.shape[-2:]
    out = jax.ShapeDtypeStruct((rows, cols), jnp.bfloat16)
    inputs, specs = [order], [SMEM]
    if pick is not None:
        inputs, specs = inputs + [pick], specs + [SMEM]
    sources = [matrix] if other is None else [matrix, other]
    return pl.pallas_call(
        functools.partial(split_kernel, lag, pick is not None),
        out_shape=(out, out),
        in_specs=specs + [pl.BlockSpec(memory_space=pltpu.HBM)] * len(sources),
        out_specs=(VMEM, VMEM),
        scratch_shapes=[
            pltpu.VMEM((rows, cols), jnp.float32),
            pltpu.SemaphoreType.DMA((order.shape[0],)),
        ],
        compiler_params=pltpu.CompilerParams(vmem_limit_bytes=8 << 20),
        cost_estimate=pl.CostEstimate(
            flops=0, bytes_accessed=8 * rows * cols, transcendentals=0
        ),
        name="split_blocks",
    )(*inputs, *sources)


def times(vh, vl, high_ref, low_ref):
    n = vh.shape[0]
    both = contract(high_ref[...], jnp.concatenate([vh, vl], 0))
    return both[:, :n] + both[:, n:] + contract(low_ref[...], vh)


def field_kernel(high_ref, low_ref, v_ref, base_ref, out_ref):
    out_ref[...] = base_ref[...] + times(*split_here(v_ref[...]), high_ref, low_ref).T


def costs(rows, cols, n):
    return pl.CostEstimate(
        flops=6 * rows * cols * n, bytes_accessed=4 * rows * cols, transcendentals=0
    )


def field(op, current, base):
    high, low = op
    n = current.shape[0]
    return pl.pallas_call(
        field_kernel,
        out_shape=jax.ShapeDtypeStruct((n, high.shape[0]), jnp.float32),
        in_specs=[VMEM] * 4,
        out_specs=VMEM,
        compiler_params=pltpu.CompilerParams(vmem_limit_bytes=8 << 20),
        cost_estimate=costs(*high.shape, n),
        name="field",
    )(high, low, current, base)


def lead_kernel(high_ref, low_ref, near_ref, far_ref, rest_ref, mine_ref, theirs_ref):
    v = jnp.concatenate([near_ref[...], far_ref[...]], 1)
    rhs = rest_ref[...] - times(*split_here(v), high_ref, low_ref).T
    n = mine_ref.shape[0]
    mine_ref[...] = rhs[:n]
    theirs_ref[...] = rhs[n:]


def lead(op, near, far, rest):
    high, low = op
    n = near.shape[0]
    shape = jax.ShapeDtypeStruct((n // 2, high.shape[0]), jnp.float32)
    return pl.pallas_call(
        lead_kernel,
        out_shape=(shape, shape),
        in_specs=[VMEM] * 5,
        out_specs=(VMEM, VMEM),
        compiler_params=pltpu.CompilerParams(vmem_limit_bytes=8 << 20),
        cost_estimate=costs(*high.shape, n),
        name="lead",
    )(high, low, near, far, rest)


def last_kernel(h0_ref, l0_ref, h1_ref, l1_ref, v_ref, b0_ref, b1_ref, current_ref, out_ref):
    rows = current_ref.shape[0]
    vh, vl = split_here(v_ref[...])
    current_ref[...] = v_ref[:, :rows].T
    out_ref[0] = b0_ref[...].T + times(vh, vl, h0_ref, l0_ref)
    out_ref[1] = b1_ref[...].T + times(vh, vl, h1_ref, l1_ref)


def last(op0, op1, current, base0, base1):
    rows, cols = op0[0].shape
    n = current.shape[0]
    return pl.pallas_call(
        last_kernel,
        out_shape=(
            jax.ShapeDtypeStruct((rows, n), jnp.float32),
            jax.ShapeDtypeStruct((2, rows, n), jnp.float32),
        ),
        in_specs=[VMEM] * 7,
        out_specs=(VMEM, VMEM),
        compiler_params=pltpu.CompilerParams(vmem_limit_bytes=8 << 20),
        cost_estimate=costs(2 * rows, cols, n),
        name="last",
    )(*op0, *op1, current, base0, base1)


def quad_body(lag_ops, inverse, history, loads):
    rows_n = lax.axis_size("row")
    height = lag_ops.shape[1]
    width = loads.shape[2] // 4
    g = lax.axis_index("lag")
    r = lax.axis_index("row")
    first_plane, first_core = g < 2, (g & 1) == 0
    near = [k for k in range(0, rows_n, 2)]
    steps = near + [k + 1 for k in near]
    cut = len(near) * height
    order = r ^ jnp.array(steps, jnp.int32)

    tie = lax.optimization_barrier

    def line(v):
        parts = [v]
        for k in near[1:]:
            parts.append(swap(v, 0, k))
        return jnp.concatenate(parts, 1)

    def scatter(rhs):
        parts = [rhs[j * width : (j + 1) * width] for j in range(4)]
        got = [parts[0]] + [swap(parts[j], j, 0) for j in (3, 2, 1)][::-1]
        return lax.select_n(g, *got)

    def exchange(a):
        near_y = swap(a, 2, 0)
        far_y = swap(a, 2, 1)
        far = swap(a, 0, 1)
        return jnp.concatenate([a, near_y], 0), jnp.concatenate([far, far_y], 0)

    def full(near_, far_):
        v = jnp.concatenate([near_, far_], 1)
        w = jnp.concatenate([swap(near_, 1, 0), swap(far_, 1, 0)], 1)
        chunks = [v[:width], w[:width], v[width:], w[width:]]
        even = [jnp.where(first_core, chunks[j], chunks[j ^ 1]) for j in range(4)]
        return jnp.concatenate(
            [jnp.where(first_plane, even[j], even[j ^ 2]) for j in range(4)], 0
        )

    def behind(array):
        return swap(array, 1, 0), swap(array, 3, 0)

    def choose(received):
        near_, far = received
        return jnp.where(first_core, near_, jnp.where(first_plane, far, 0.0))

    def pick(array, j):
        return jnp.concatenate([array[(j + k) * width : (j + k + 1) * width] for k in (0, 2)], 0)

    def pair(array):
        return jnp.where(first_core, pick(array, 0), swap(pick(array, 1), 1, 0))

    keep = functools.partial(pltpu.with_memory_space_constraint, memory_space=pltpu.HBM)
    acc0, rhs = turn_first(keep(history), keep(loads))
    rhs, first_plane, first_core, g = tie((rhs, first_plane, first_core, g))
    which = (g & 1).reshape(1)
    rhs = scatter(rhs)
    rhs, acc0, sent_ops = tie((rhs, acc0, lag_ops))
    other_ops = swap(sent_ops, 1, 0)
    for step in range(STEPS):
        if step == 0:
            rhs, order, which = tie((rhs, order, which))
            high, low = split_blocks(keep(inverse), order)
            inv = [(high[:, :cut], low[:, :cut]), (high[:, cut:], low[:, cut:])]
            a = line(rhs)
            a, inv = tie((a, inv))
            acc1, given = turn(history, loads)
            a, order = tie((a, order))
            own1 = split_blocks(keep(lag_ops), order, 1)
            b = swap(a, 0, 1)
            b, acc1, given, own1 = tie((b, acc1, given, own1))
        else:
            current = full(near_, far_)
            rhs, received = tie((rhs, received))
            below = choose(received)
            new0 = field(own0, current, acc1)
            a = line(rhs)
            a, acc0, current = tie((a, new0, current))
            acc1 = field(own1, current, below)
            b = swap(a, 0, 1)
            b, acc1 = tie((b, acc1))
        received = behind(acc0)
        solved = field(inv[1], b, product(split(a), inv[0]))
        a = line(solved)
        if step < STEPS - 1:
            led = pair(acc1)
            rest = jnp.where(first_core, pick(given[step], 0), pick(given[step], 1)) - led
        if step == 0:
            a, order, which = tie((a, order, which))
            first = split_blocks(keep(lag_ops), order, 0, which, keep(other_ops))
            own0 = split_blocks(keep(lag_ops), order, 0)
        near_, far_ = exchange(a)
        if step == 0:
            near_, far_, own0, first = tie((near_, far_, own0, first))
        if step < STEPS - 1:
            near_, far_, rest = tie((near_, far_, rest))
            mine, theirs = lead(first, near_, far_, rest)
            rhs = jnp.where(first_plane, mine, swap(theirs, 2, 0))
    current = full(near_, far_)
    return last(own0, own1, current, acc1, choose(received))


def solution(mesh):
    placed = (P("lag", "row", None), P("row", None), P("lag", "row", None), P(None, "row", None))

    def body(lag_ops, inverse, history, loads):
        lags, rows = lax.axis_size("lag"), lax.axis_size("row")
        fits = (
            lags == 4
            and lag_ops.shape[0] == STEPS - 1
            and rows & (rows - 1) == 0
            and lag_ops.shape[1] * rows == lag_ops.shape[2]
            and loads.shape[0] == STEPS
        )
        return (quad_body if fits else plain_body)(lag_ops, inverse, history, loads)

    return jax.shard_map(
        body,
        mesh=mesh,
        in_specs=placed,
        out_specs=(P("row", None), P("lag", "row", None)),
        check_vma=False,
    )
```

```python
import functools

import jax
import jax.numpy as jnp
from jax import lax
from jax.experimental import pallas as pl
from jax.experimental.pallas import tpu as pltpu
from jax.sharding import PartitionSpec as P


STEPS = 3
AXES = ("lag", "row")


def broadcast(array, axis, root):
    mine = lax.axis_index(axis) == root
    return lax.psum(jnp.where(mine, array, jnp.zeros_like(array)), axis)


def from_behind(array, axis, by):
    length = lax.axis_size(axis)
    pairs = [(i, i + by) for i in range(length) if 0 <= i + by < length]
    return lax.ppermute(array, axis, pairs)


def plain_body(lag_ops, inverse, history, loads):
    acc = history
    local_lags = lag_ops.shape[0]
    local_rows = lag_ops.shape[1]
    total_cols = lag_ops.shape[2]
    loads_width = history.shape[2]
    flat_ops = lag_ops.reshape(local_lags * local_rows, total_cols)
    current = jnp.zeros((local_rows, loads_width), jnp.float32)
    for step in range(STEPS):
        rhs = broadcast(loads[step] - acc[0], "lag", 0)
        width = loads_width // lax.axis_size("lag")
        offset = lax.axis_index("lag") * width
        rhs_part = lax.dynamic_slice_in_dim(rhs, offset, width, 1)
        partial_value = jnp.dot(
            inverse,
            lax.all_gather(rhs_part, "row", axis=0, tiled=True),
            precision=lax.Precision.HIGHEST,
            preferred_element_type=jnp.float32,
        )
        current = lax.all_gather(partial_value, "lag", axis=1, tiled=True)
        product = jnp.dot(
            flat_ops,
            lax.all_gather(current, "row", axis=0, tiled=True),
            precision=lax.Precision.HIGHEST,
            preferred_element_type=jnp.float32,
        )
        product = product.reshape(local_lags, local_rows, loads_width)
        incoming = from_behind(acc[0], "lag", -1)
        shifted = jnp.concatenate([acc[1:], incoming[None]], axis=0)
        acc = shifted + product
    return (current, acc)


def swap(array, lag_bits, row_bits):
    lags, rows = lax.axis_size("lag"), lax.axis_size("row")
    pairs = [
        (g * rows + r, (g ^ lag_bits) * rows + (r ^ row_bits))
        for g in range(lags)
        for r in range(rows)
    ]
    return lax.ppermute(array, AXES, pairs)


def split(array):
    high = lax.reduce_precision(array, 8, 7)
    return high.astype(jnp.bfloat16), (array - high).astype(jnp.bfloat16)


def split_here(array):
    high = array.astype(jnp.bfloat16)
    return high, (array - high.astype(jnp.float32)).astype(jnp.bfloat16)


def contract(a, b):
    return lax.dot_general(
        a, b, (((1,), (1,)), ((), ())), preferred_element_type=jnp.float32
    )


def product(vector, matrix):
    vh, vl = vector
    mh, ml = matrix
    n = vh.shape[0]
    both = contract(jnp.concatenate([vh, vl], 0), mh)
    return both[:n] + both[n:] + contract(vh, ml)


VMEM = pl.BlockSpec(memory_space=pltpu.VMEM)
SMEM = pl.BlockSpec(memory_space=pltpu.SMEM)


def turn_first_kernel(history_ref, loads_ref, past_ref, rhs_ref):
    past_ref[...] = history_ref[0].T
    rhs_ref[...] = loads_ref[0].T - past_ref[...]


def turn_first(history, loads):
    _, rows, n = history.shape
    spec = pl.BlockSpec((1, rows, n), lambda i: (0, 0, 0))
    shape = jax.ShapeDtypeStruct((n, rows), history.dtype)
    out = pl.BlockSpec((n, rows), lambda i: (0, 0))
    return pl.pallas_call(
        turn_first_kernel,
        out_shape=(shape, shape),
        grid=(1,),
        in_specs=[spec, spec],
        out_specs=(out, out),
        compiler_params=pltpu.CompilerParams(vmem_limit_bytes=8 << 20),
        name="turn_first",
    )(history, loads)


def turn_kernel(history_ref, loads_ref, past_ref, given_ref):
    past_ref[...] = history_ref[1].T
    for i in range(given_ref.shape[0]):
        given_ref[i] = loads_ref[i + 1].T


def turn(history, loads):
    _, rows, n = history.shape
    return pl.pallas_call(
        turn_kernel,
        out_shape=(
            jax.ShapeDtypeStruct((n, rows), history.dtype),
            jax.ShapeDtypeStruct((loads.shape[0] - 1, n, rows), loads.dtype),
        ),
        compiler_params=pltpu.CompilerParams(vmem_limit_bytes=8 << 20),
        name="turn",
    )(history, loads)


def split_kernel(lag, picks, order_ref, *refs):
    high_ref, low_ref, buffer, arrived = refs[-4:]
    size = buffer.shape[1] // order_ref.shape[0]

    def copies(source_ref):
        view = source_ref if lag is None else source_ref.at[lag]
        return [
            pltpu.make_async_copy(
                view.at[:, pl.ds(pl.multiple_of(order_ref[i] * size, 128), size)],
                buffer.at[:, pl.ds(i * size, size)],
                arrived.at[i],
            )
            for i in range(order_ref.shape[0])
        ]

    if picks:
        pick_ref, first_ref, second_ref = refs[:3]

        @pl.when(pick_ref[0] == 0)
        def _():
            for copy in copies(first_ref):
                copy.start()

        @pl.when(pick_ref[0] != 0)
        def _():
            for copy in copies(second_ref):
                copy.start()
    else:
        first_ref = refs[0]
        for copy in copies(first_ref):
            copy.start()
    for i, copy in enumerate(copies(first_ref)):
        copy.wait()
        part = pl.ds(i * size, size)
        high_ref[:, part], low_ref[:, part] = split_here(buffer[:, part])


def split_blocks(matrix, order, lag=None, pick=None, other=None):
    rows, cols = matrix.shape[-2:]
    out = jax.ShapeDtypeStruct((rows, cols), jnp.bfloat16)
    inputs, specs = [order], [SMEM]
    if pick is not None:
        inputs, specs = inputs + [pick], specs + [SMEM]
    sources = [matrix] if other is None else [matrix, other]
    return pl.pallas_call(
        functools.partial(split_kernel, lag, pick is not None),
        out_shape=(out, out),
        in_specs=specs + [pl.BlockSpec(memory_space=pltpu.HBM)] * len(sources),
        out_specs=(VMEM, VMEM),
        scratch_shapes=[
            pltpu.VMEM((rows, cols), jnp.float32),
            pltpu.SemaphoreType.DMA((order.shape[0],)),
        ],
        compiler_params=pltpu.CompilerParams(vmem_limit_bytes=8 << 20),
        cost_estimate=pl.CostEstimate(
            flops=0, bytes_accessed=8 * rows * cols, transcendentals=0
        ),
        name="split_blocks",
    )(*inputs, *sources)


def times(vh, vl, high_ref, low_ref):
    n = vh.shape[0]
    both = contract(high_ref[...], jnp.concatenate([vh, vl], 0))
    return both[:, :n] + both[:, n:] + contract(low_ref[...], vh)


def field_kernel(high_ref, low_ref, v_ref, base_ref, out_ref):
    out_ref[...] = base_ref[...] + times(*split_here(v_ref[...]), high_ref, low_ref).T


def costs(rows, cols, n):
    return pl.CostEstimate(
        flops=6 * rows * cols * n, bytes_accessed=4 * rows * cols, transcendentals=0
    )


def field(op, current, base):
    high, low = op
    n = current.shape[0]
    return pl.pallas_call(
        field_kernel,
        out_shape=jax.ShapeDtypeStruct((n, high.shape[0]), jnp.float32),
        in_specs=[VMEM] * 4,
        out_specs=VMEM,
        compiler_params=pltpu.CompilerParams(vmem_limit_bytes=8 << 20),
        cost_estimate=costs(*high.shape, n),
        name="field",
    )(high, low, current, base)


def lead_kernel(columns, high_ref, low_ref, v_ref, rest_ref, *out_refs):
    high_ref, low_ref = high_ref.at[:, columns], low_ref.at[:, columns]
    rhs = rest_ref[...] - times(*split_here(v_ref[...]), high_ref, low_ref).T
    if len(out_refs) == 1:
        out_refs[0][...] = rhs
    else:
        n = out_refs[0].shape[0]
        out_refs[0][...] = rhs[:n]
        out_refs[1][...] = rhs[n:]


def lead(op, columns, current, rest, parts):
    high, low = op
    rows, n = high.shape[0], current.shape[0]
    shape = jax.ShapeDtypeStruct((n // parts, rows), jnp.float32)
    return pl.pallas_call(
        functools.partial(lead_kernel, columns),
        out_shape=(shape,) * parts,
        in_specs=[VMEM] * 4,
        out_specs=(VMEM,) * parts,
        compiler_params=pltpu.CompilerParams(vmem_limit_bytes=8 << 20),
        cost_estimate=costs(rows, current.shape[1], n),
        name="lead",
    )(high, low, current, rest)


def last_near_kernel(columns, h0_ref, l0_ref, h1_ref, l1_ref, v_ref, b0_ref, b1_ref, current_ref, out_ref):
    rows = current_ref.shape[0]
    vh, vl = split_here(v_ref[...])
    current_ref[...] = v_ref[:, :rows].T
    sides = (h0_ref, l0_ref, b0_ref), (h1_ref, l1_ref, b1_ref)
    for i, (h_ref, l_ref, b_ref) in enumerate(sides):
        out_ref[i] = b_ref[...].T + times(vh, vl, h_ref.at[:, columns], l_ref.at[:, columns])


def last_far_kernel(columns, h0_ref, l0_ref, h1_ref, l1_ref, v_ref, base_ref, out_ref):
    vh, vl = split_here(v_ref[...])
    for i, (h_ref, l_ref) in enumerate(((h0_ref, l0_ref), (h1_ref, l1_ref))):
        out_ref[i] = base_ref[i] + times(vh, vl, h_ref.at[:, columns], l_ref.at[:, columns])


def last_near(op0, op1, columns, current, base0, base1):
    rows, n = op0[0].shape[0], current.shape[0]
    return pl.pallas_call(
        functools.partial(last_near_kernel, columns),
        out_shape=(
            jax.ShapeDtypeStruct((rows, n), jnp.float32),
            jax.ShapeDtypeStruct((2, rows, n), jnp.float32),
        ),
        in_specs=[VMEM] * 7,
        out_specs=(VMEM, VMEM),
        compiler_params=pltpu.CompilerParams(vmem_limit_bytes=8 << 20),
        cost_estimate=costs(2 * rows, current.shape[1], n),
        name="last_near",
    )(*op0, *op1, current, base0, base1)


def last_far(op0, op1, columns, current, base):
    rows, n = op0[0].shape[0], current.shape[0]
    return pl.pallas_call(
        functools.partial(last_far_kernel, columns),
        out_shape=jax.ShapeDtypeStruct((2, rows, n), jnp.float32),
        in_specs=[VMEM] * 6,
        out_specs=VMEM,
        compiler_params=pltpu.CompilerParams(vmem_limit_bytes=8 << 20),
        cost_estimate=costs(2 * rows, current.shape[1], n),
        name="last_far",
    )(*op0, *op1, current, base)


def quad_body(lag_ops, inverse, history, loads):
    rows_n = lax.axis_size("row")
    height = lag_ops.shape[1]
    width = loads.shape[2] // 4
    g = lax.axis_index("lag")
    r = lax.axis_index("row")
    first_plane, first_core = g < 2, (g & 1) == 0
    near = [k for k in range(0, rows_n, 2)]
    steps = near + [k + 1 for k in near]
    cut = len(near) * height
    order = r ^ jnp.array(steps, jnp.int32)

    near_columns, far_columns = pl.ds(0, cut), pl.ds(cut, cut)
    tie = lax.optimization_barrier

    def line(v):
        parts = [v]
        for k in near[1:]:
            parts.append(swap(v, 0, k))
        return jnp.concatenate(parts, 1)

    def scatter(rhs):
        parts = [rhs[j * width : (j + 1) * width] for j in range(4)]
        got = [parts[0]] + [swap(parts[j], j, 0) for j in (3, 2, 1)][::-1]
        return lax.select_n(g, *got)

    def exchange(a):
        near_y = swap(a, 2, 0)
        far_y = swap(a, 2, 1)
        far = swap(a, 0, 1)
        return jnp.concatenate([a, near_y], 0), jnp.concatenate([far, far_y], 0)

    def full(v):
        w = swap(v, 1, 0)
        chunks = [v[:width], w[:width], v[width:], w[width:]]
        even = [jnp.where(first_core, chunks[j], chunks[j ^ 1]) for j in range(4)]
        return jnp.concatenate(
            [jnp.where(first_plane, even[j], even[j ^ 2]) for j in range(4)], 0
        )

    def behind(array):
        return swap(array, 1, 0), swap(array, 3, 0)

    def choose(received):
        near_, far = received
        return jnp.where(first_core, near_, jnp.where(first_plane, far, 0.0))

    def pick(array, j):
        return jnp.concatenate([array[(j + k) * width : (j + k + 1) * width] for k in (0, 2)], 0)

    def pair(array):
        return jnp.where(first_core, pick(array, 0), swap(pick(array, 1), 1, 0))

    keep = functools.partial(pltpu.with_memory_space_constraint, memory_space=pltpu.HBM)
    acc0, rhs = turn_first(keep(history), keep(loads))
    rhs, first_plane, first_core, g = tie((rhs, first_plane, first_core, g))
    which = (g & 1).reshape(1)
    rhs = scatter(rhs)
    rhs, acc0, sent_ops = tie((rhs, acc0, lag_ops))
    other_ops = swap(sent_ops, 1, 0)
    for step in range(STEPS):
        if step == 0:
            rhs, order, which = tie((rhs, order, which))
            high, low = split_blocks(keep(inverse), order)
            inv = [(high[:, :cut], low[:, :cut]), (high[:, cut:], low[:, cut:])]
            a = line(rhs)
            a, inv = tie((a, inv))
            acc1, given = turn(history, loads)
            a, order = tie((a, order))
            own1 = split_blocks(keep(lag_ops), order, 1)
            b = swap(a, 0, 1)
            b, acc1, given, own1 = tie((b, acc1, given, own1))
        else:
            current = jnp.concatenate([full(near_), full(far_)], 1)
            rhs, received = tie((rhs, received))
            below = choose(received)
            new0 = field(own0, current, acc1)
            a = line(rhs)
            a, acc0, current = tie((a, new0, current))
            acc1 = field(own1, current, below)
            b = swap(a, 0, 1)
            b, acc1 = tie((b, acc1))
        received = behind(acc0)
        solved = field(inv[1], b, product(split(a), inv[0]))
        a = line(solved)
        if step < STEPS - 1:
            led = pair(acc1)
            rest = jnp.where(first_core, pick(given[step], 0), pick(given[step], 1)) - led
        if step == 0:
            a, order, which = tie((a, order, which))
            first = split_blocks(keep(lag_ops), order, 0, which, keep(other_ops))
            own0 = split_blocks(keep(lag_ops), order, 0)
        near_, far_ = exchange(a)
        if step == 0:
            near_, own0, first = tie((near_, own0, first))
        if step < STEPS - 1:
            near_, rest = tie((near_, rest))
            (rest,) = lead(first, near_columns, near_, rest, 1)
            far_, rest = tie((far_, rest))
            mine, theirs = lead(first, far_columns, far_, rest, 2)
            rhs = jnp.where(first_plane, mine, swap(theirs, 2, 0))
    current = full(near_)
    current, future = last_near(own0, own1, near_columns, current, acc1, choose(received))
    far_ = full(far_)
    return current, last_far(own0, own1, far_columns, far_, future)


def solution(mesh):
    placed = (P("lag", "row", None), P("row", None), P("lag", "row", None), P(None, "row", None))

    def body(lag_ops, inverse, history, loads):
        lags, rows = lax.axis_size("lag"), lax.axis_size("row")
        fits = (
            lags == 4
            and lag_ops.shape[0] == STEPS - 1
            and rows & (rows - 1) == 0
            and lag_ops.shape[1] * rows == lag_ops.shape[2]
            and loads.shape[0] == STEPS
        )
        return (quad_body if fits else plain_body)(lag_ops, inverse, history, loads)

    return jax.shard_map(
        body,
        mesh=mesh,
        in_specs=placed,
        out_specs=(P("row", None), P("lag", "row", None)),
        check_vma=False,
    )
```
